32 devices in a mesh: seq: 16 (over z, y, core), head: 2 (over x).
Axes of the slice: x: 2, y: 2, z: 4, core: 2. Of those that a mesh axis runs over, the one named last changes fastest.
Arguments:
- tokens: bfloat16 [8192, 2048], P('seq', 'head'), may hold values from -200 to 200
- norm_gain: float32 [2, 2048], replicated, may hold values from 0.25 to 1.75
- w_query: bfloat16 [2, 2048, 2048], P(None, None, 'head'), may hold values from -0.35 to 0.35
- key_projection_weight: bfloat16 [2, 2048, 512], P(None, None, 'head'), may hold values from -0.35 to 0.35
- value_projection_weight: bfloat16 [2, 2048, 512], P(None, None, 'head'), may hold values from -0.125 to 0.125
- w_out: bfloat16 [2, 2048, 2048], P(None, 'head'), may hold values from -0.125 to 0.125
- counts: int32 [16], replicated, may hold values from 128 to 512
Outputs:
- hidden_out: bfloat16 [8192, 2048], P('seq', 'head')
The draws below stay inside these ranges and needn't reach their ends.
Inputs may be any that keep to these rules, and one draw needn't show every extreme that they name: The first counts[b] tokens of block b of 512 positions are valid keys; the rest of the block is padding that no query uses as a key.
All inputs are finite; a program needn't handle non-finite values.
Results may differ from the reference program's by a relative error of at most 0.02.
The reference program's roundings to bfloat16 on the way count: a program that leaves them out, or rounds other values in their place, can miss the bound.
Values may be sent and summed in bfloat16 or wider, within the bound.
A program may use at most 128 MiB of HBM per device.

```python
import math
import jax
import jax.numpy as jnp
from jax import lax

MODEL_WIDTH = 2048
QUERY_HEAD_COUNT = 16
KEY_VALUE_HEADS = 4
HEAD_SIZE = 128
WINDOW = 4096
LAYER_COUNT = 2
BLOCK_TOKENS = 512
BLOCKS = 16
SEQUENCE_TOKENS = 8192
N_HEAD = 2


def sample_projection(key, salt, columns):
    scale_value = 1.6 / math.sqrt(MODEL_WIDTH)
    inner = jax.random.fold_in(key, salt)
    sampled_values = scale_value * jax.random.normal(inner, (LAYER_COUNT, MODEL_WIDTH, columns), jnp.float32)
    return jnp.clip(sampled_values, -0.35, 0.35)


def draw_w_query(key, part):
    sampled_values = sample_projection(key, 101, QUERY_HEAD_COUNT * HEAD_SIZE)
    return sampled_values.astype(jnp.bfloat16)


def draw_key_projection_weight(key, part):
    sampled_values = sample_projection(key, 102, KEY_VALUE_HEADS * HEAD_SIZE)
    return sampled_values.astype(jnp.bfloat16)


def draw_tokens(key, part):
    inner = jax.random.fold_in(key, 201)
    values = jnp.clip(jax.random.normal(inner, (SEQUENCE_TOKENS, MODEL_WIDTH), jnp.float32), -6.0, 6.0)
    return values.astype(jnp.bfloat16)


def set_ends(entries, rng, smallest, top_value):
    index_at = [jax.random.randint(jax.random.fold_in(rng, axis), (), 0, length) for axis, length in enumerate(entries.shape)]
    longest = entries.shape.index(max(entries.shape))
    next_to = index_at[:longest] + [(index_at[longest] + 1) % entries.shape[longest]] + index_at[longest + 1:]
    return entries.at[tuple(index_at)].set(smallest).at[tuple(next_to)].set(top_value)


def levels(key, dims, pieces, smallest, top_value):
    factor_of, own = 1.0, jax.random.fold_in(key, 6)
    for dim, shards_of in pieces:
        steps = jnp.exp(jax.random.uniform(jax.random.fold_in(own, dim), (shards_of,), jnp.float32, smallest / len(pieces), top_value / len(pieces)))
        factor_of = factor_of * jnp.repeat(steps, dims[dim] // shards_of).reshape([-1 if axis == dim else 1 for axis in range(len(dims))])
    return factor_of


def normal_values(stream_key, dims, width, most, pieces=(), kind=jnp.bfloat16):
    result = width * jax.random.normal(stream_key, dims, jnp.float32)
    if pieces:
        result = result * levels(stream_key, dims, pieces, -0.22, 0.18)
    return jnp.clip(result, -most, most).astype(kind)


def setup_inputs(seed: int = 0) -> dict:
    keys = jax.random.split(jax.random.key(seed), 8)
    return {
        "tokens": draw_tokens(jax.random.fold_in(keys[7], 71), 0),
        "norm_gain": jnp.clip(1.0 + 0.15 * jax.random.normal(keys[1], (LAYER_COUNT, MODEL_WIDTH), jnp.float32), 0.25, 1.75),
        "w_query": draw_w_query(jax.random.fold_in(keys[7], 71), 0),
        "key_projection_weight": draw_key_projection_weight(jax.random.fold_in(keys[7], 71), 0),
        "value_projection_weight": normal_values(keys[4], (LAYER_COUNT, MODEL_WIDTH, KEY_VALUE_HEADS * HEAD_SIZE), MODEL_WIDTH ** -0.5, 0.125, ((2, 2),)),
        "w_out": normal_values(keys[5], (LAYER_COUNT, QUERY_HEAD_COUNT * HEAD_SIZE, MODEL_WIDTH), (QUERY_HEAD_COUNT * HEAD_SIZE) ** -0.5, 0.125, ((1, 2),)),
        "counts": set_ends(jax.random.randint(keys[6], (BLOCKS,), BLOCK_TOKENS // 4, BLOCK_TOKENS + 1), jax.random.fold_in(keys[6], 1), BLOCK_TOKENS // 4, BLOCK_TOKENS).astype(jnp.int32),
    }


norm_epsilon = 1e-05
rope_base = 10000.0

def rms_norm(hidden, gain_row):
    widened = hidden.astype(jnp.float32)
    mean_square = lax.optimization_barrier(jnp.mean(widened * widened, axis=-1, keepdims=True))
    scaled = widened * lax.rsqrt(mean_square + norm_epsilon) * gain_row.astype(jnp.float32)
    return scaled.astype(jnp.bfloat16)

def apply_rotary_embedding(projected, token_positions, head_count):
    row_total = projected.shape[0]
    shaped = projected.reshape(row_total, head_count, HEAD_SIZE)
    half_dim = HEAD_SIZE // 2
    inverse = jnp.power(jnp.float32(rope_base), -2.0 * jnp.arange(half_dim, dtype=jnp.float32) / HEAD_SIZE)
    angles = token_positions.astype(jnp.float32)[:, None] * inverse[None, :]
    cosine_table = jnp.cos(angles)[:, None, :]
    sine_table = jnp.sin(angles)[:, None, :]
    first_half = shaped[..., :half_dim]
    second_half = shaped[..., half_dim:]
    rotated = jnp.concatenate([first_half * cosine_table - second_half * sine_table, second_half * cosine_table + first_half * sine_table], axis=-1)
    return rotated.astype(jnp.bfloat16)

def key_validity(key_positions, counts):
    key_block = jnp.floor_divide(key_positions, BLOCK_TOKENS)
    within_block = key_positions - key_block * BLOCK_TOKENS
    block_count = counts[jnp.clip(key_block, 0, BLOCKS - 1)]
    return (key_positions >= 0) & (within_block < block_count)

def attend(queries, key_rows_full, value_rows_full, counts):
    span_blocks = WINDOW // BLOCK_TOKENS
    group_length = QUERY_HEAD_COUNT // KEY_VALUE_HEADS
    padding_rows = span_blocks * BLOCK_TOKENS
    key_rows_padded = jnp.concatenate([jnp.zeros((padding_rows, KEY_VALUE_HEADS, HEAD_SIZE), jnp.bfloat16), key_rows_full], axis=0)
    value_rows_padded = jnp.concatenate([jnp.zeros((padding_rows, KEY_VALUE_HEADS, HEAD_SIZE), jnp.bfloat16), value_rows_full], axis=0)
    key_length = (span_blocks + 1) * BLOCK_TOKENS
    scale_factor = 1.0 / math.sqrt(HEAD_SIZE)

    def one_block(block_index):
        first_row = block_index * BLOCK_TOKENS
        block_of_queries = lax.dynamic_slice_in_dim(queries, first_row, BLOCK_TOKENS, 0)
        key_block = lax.dynamic_slice_in_dim(key_rows_padded, first_row, key_length, 0)
        value_block = lax.dynamic_slice_in_dim(value_rows_padded, first_row, key_length, 0)
        query_positions = first_row + jnp.arange(BLOCK_TOKENS, dtype=jnp.int32)
        key_positions = first_row - padding_rows + jnp.arange(key_length, dtype=jnp.int32)
        allowed = key_validity(key_positions, counts)[None, :]
        allowed = allowed & (key_positions[None, :] <= query_positions[:, None])
        allowed = allowed & (query_positions[:, None] - key_positions[None, :] < WINDOW)
        query_broad = block_of_queries.astype(jnp.float32).reshape(BLOCK_TOKENS, KEY_VALUE_HEADS, group_length, HEAD_SIZE)
        key_wide = key_block.astype(jnp.float32)
        scores = jnp.einsum('tkgd,lkd->kgtl', query_broad, key_wide, precision=lax.Precision.HIGHEST) * scale_factor
        scores = jnp.where(allowed[None, None], scores, -jnp.inf)
        largest = lax.optimization_barrier(jnp.max(scores, axis=-1, keepdims=True))
        weights = jnp.exp(scores - largest)
        weights = (weights / lax.optimization_barrier(jnp.sum(weights, axis=-1, keepdims=True))).astype(jnp.bfloat16)
        blended = jnp.einsum('kgtl,lkd->tkgd', weights.astype(jnp.float32), value_block.astype(jnp.float32), precision=lax.Precision.HIGHEST)
        return blended.astype(jnp.bfloat16).reshape(BLOCK_TOKENS, QUERY_HEAD_COUNT * HEAD_SIZE)
    outputs = lax.map(one_block, jnp.arange(BLOCKS, dtype=jnp.int32))
    return outputs.reshape(BLOCKS * BLOCK_TOKENS, QUERY_HEAD_COUNT * HEAD_SIZE)

def reference(tokens, norm_gain, w_query, key_projection_weight, value_projection_weight, w_out, counts):
    hidden = tokens
    token_positions = jnp.arange(SEQUENCE_TOKENS, dtype=jnp.int32)
    group_width = QUERY_HEAD_COUNT * HEAD_SIZE // N_HEAD
    for layer_position in range(LAYER_COUNT):
        normalized_rows = rms_norm(hidden, norm_gain[layer_position])
        queries = apply_rotary_embedding(jnp.dot(normalized_rows, w_query[layer_position], preferred_element_type=jnp.float32), token_positions, QUERY_HEAD_COUNT)
        key_rows_full = apply_rotary_embedding(jnp.dot(normalized_rows, key_projection_weight[layer_position], preferred_element_type=jnp.float32), token_positions, KEY_VALUE_HEADS)
        value_rows_full = jnp.dot(normalized_rows, value_projection_weight[layer_position], preferred_element_type=jnp.float32).astype(jnp.bfloat16).reshape(SEQUENCE_TOKENS, KEY_VALUE_HEADS, HEAD_SIZE)
        attended = attend(queries, key_rows_full, value_rows_full, counts)
        branch = jnp.zeros((SEQUENCE_TOKENS, MODEL_WIDTH), jnp.float32)
        for group_index in range(N_HEAD):
            column_start = group_index * group_width
            partial_product = jnp.dot(attended[:, column_start:column_start + group_width], w_out[layer_position, column_start:column_start + group_width], preferred_element_type=jnp.float32)
            rounded = lax.optimization_barrier(partial_product.astype(jnp.bfloat16))
            branch = branch + rounded.astype(jnp.float32)
        hidden = (hidden.astype(jnp.float32) + branch).astype(jnp.bfloat16)
    return hidden
```

```python
import functools
import math

import jax
import jax.numpy as jnp
from jax import lax
from jax.experimental import pallas as pl
from jax.experimental.pallas import tpu as pltpu
from jax.sharding import PartitionSpec as P

HEAD_SIZE = 128
WINDOW = 4096
CHUNKS = 1
KEY_TILE = 512
FLAG_COLUMNS = 16

norm_epsilon = 1e-05
rope_base = 10000.0


def moved(value, axis, target_of):
    count = lax.axis_size(axis)
    pairs = [(source, target_of(source)) for source in range(count)]
    return lax.ppermute(value, axis, [(a, b) for a, b in pairs if 0 <= b < count])


def spread_blocks(own, span):
    if span != 8 or lax.axis_size("seq") % 4:
        blocks = [own]
        for _ in range(span):
            blocks.append(moved(blocks[-1], "seq", lambda i: i + 1))
        return blocks
    index = lax.axis_index("seq")
    low_chip = index % 4 < 2
    first_core = index % 2 == 0
    pick_chip = lambda a, b: jnp.where(low_chip, a, b)
    pick_core = lambda a, b: jnp.where(first_core, a, b)
    across = lambda i: i + 2 if i % 4 < 2 else i - 2
    beside = lambda i: i + 1 if i % 2 == 0 else i - 1
    four = moved(own, "seq", lambda i: i + 4)
    eight = moved(own, "seq", lambda i: i + 8)
    two = moved(pick_chip(own, four), "seq", across)
    six = moved(pick_chip(four, eight), "seq", across)
    one = moved(pick_core(own, two), "seq", beside)
    three = moved(pick_core(two, four), "seq", beside)
    five = moved(pick_core(four, six), "seq", beside)
    seven = moved(pick_core(six, eight), "seq", beside)
    return [own, one, two, three, four, five, six, seven, eight]


def attention_kernel(span, groups, group_length, *refs):
    counts_ref, q_ref = refs[:2]
    blocks = refs[2 : 3 + span]
    o_ref, kp, vp, acc, top = refs[3 + span :]
    rows = blocks[0].shape[0]
    queries = q_ref.shape[1]
    width = groups * HEAD_SIZE
    half = min(256, queries)
    offset = jnp.int32(0)

    def flags(count, first, size, columns):
        places = first + lax.broadcasted_iota(jnp.int32, (size, columns), 0)
        return (places < count).astype(jnp.float32).astype(jnp.bfloat16)

    def store(at, size, keys, values, flag):
        where = pl.ds(pl.multiple_of(at, 16), size)
        kp[where, :] = keys
        for g in range(groups):
            vp[where, 2 * g * HEAD_SIZE : (2 * g + 1) * HEAD_SIZE] = values(g)
            vp[where, (2 * g + 1) * HEAD_SIZE : (2 * g + 2) * HEAD_SIZE] = flag

    for d in range(1, span):
        count = counts_ref[d]
        store(
            offset,
            rows,
            blocks[d][:, :width],
            lambda g: blocks[d][:, width + g * HEAD_SIZE : width + (g + 1) * HEAD_SIZE],
            flags(count, 0, rows, HEAD_SIZE),
        )
        offset = offset + ((count + 15) // 16) * 16
    blank = jnp.zeros((KEY_TILE, HEAD_SIZE), jnp.bfloat16)
    store(
        offset,
        KEY_TILE,
        jnp.broadcast_to(blocks[0][0:1, :width], (KEY_TILE, width)),
        lambda g: blank,
        blank,
    )
    tiles = (offset + KEY_TILE - 1) // KEY_TILE

    def step(g, keys, values, mask_of, skip):
        for head in range(group_length):
            head_rows = slice((g * group_length + head) * HEAD_SIZE, (g * group_length + head + 1) * HEAD_SIZE)
            for part in range(queries // half):
                if skip(part):
                    continue
                columns = slice(part * half, (part + 1) * half)
                spot = slice(head * queries + part * half, head * queries + (part + 1) * half)
                scores = jnp.dot(keys, q_ref[head_rows, columns], preferred_element_type=jnp.float32)
                mask = mask_of(part)
                if mask is not None:
                    scores = jnp.where(mask, scores, -jnp.inf)
                before = top[0:1, spot]
                after = jnp.maximum(before, jnp.max(scores, axis=0, keepdims=True))
                weights = jnp.exp2(scores - after).astype(jnp.bfloat16)
                fade = jnp.exp2(before - after)
                added = lax.dot_general(
                    values, weights, (((0,), (0,)), ((), ())), preferred_element_type=jnp.float32
                )
                acc[:, spot] = acc[:, spot] * fade + added
                top[0:1, spot] = after

    def edge_values(d, g, first):
        block = blocks[d][first : first + half, width + g * HEAD_SIZE : width + (g + 1) * HEAD_SIZE]
        return jnp.concatenate([block, flags(counts_ref[d], first, half, FLAG_COLUMNS)], axis=1)

    key_place = lax.broadcasted_iota(jnp.int32, (half, half), 0)
    query_place = lax.broadcasted_iota(jnp.int32, (half, half), 1)
    shift = counts_ref[span + 1]
    first_part = 0

    for g in range(groups):
        lanes = slice(g * HEAD_SIZE, (g + 1) * HEAD_SIZE)
        acc[...] = jnp.zeros_like(acc)
        top[...] = jnp.full_like(top, -jnp.inf)
        for tile in range(rows // half):
            first = tile * half
            step(
                g,
                blocks[0][first : first + half, lanes],
                edge_values(0, g, first),
                lambda part: (key_place <= query_place) if part == tile else None,
                lambda part: tile > part,
            )

        @pl.loop(0, tiles)
        def _(i):
            where = pl.ds(pl.multiple_of(i * KEY_TILE, KEY_TILE), KEY_TILE)
            step(
                g,
                kp[where, lanes],
                vp[where, 2 * g * HEAD_SIZE : 2 * g * HEAD_SIZE + HEAD_SIZE + FLAG_COLUMNS],
                lambda part: None,
                lambda part: False,
            )

        for tile in range(rows // half):
            first = tile * half

            @pl.when(counts_ref[span] > first)
            def _():
                inside = key_place + first < counts_ref[span]
                step(
                    g,
                    blocks[span][first : first + half, lanes],
                    edge_values(span, g, first),
                    lambda part: (inside & (key_place > query_place)) if part == tile else inside,
                    lambda part: tile < part,
                )

        for head in range(group_length):
            spot = slice(head * queries, (head + 1) * queries)
            head_rows = slice((g * group_length + head) * HEAD_SIZE, (g * group_length + head + 1) * HEAD_SIZE)
            total = acc[HEAD_SIZE : HEAD_SIZE + 1, spot]
            o_ref[head_rows, :] = (acc[:HEAD_SIZE, spot] / total).astype(jnp.bfloat16)


def attend(queries_t, blocks, counts_here, groups):
    span = len(blocks) - 1
    rows = blocks[0].shape[0]
    queries = queries_t.shape[1]
    group_length = queries_t.shape[0] // HEAD_SIZE // groups
    packed = (span - 1) * rows + KEY_TILE
    vmem = pl.BlockSpec(memory_space=pltpu.VMEM)
    keys_all = span * rows * 3 // 4
    pairs = queries * keys_all * group_length * groups
    return pl.pallas_call(
        functools.partial(attention_kernel, span, groups, group_length),
        out_shape=jax.ShapeDtypeStruct(queries_t.shape, jnp.bfloat16),
        in_specs=[pl.BlockSpec(memory_space=pltpu.SMEM)] + [vmem] * (2 + span),
        out_specs=vmem,
        scratch_shapes=[
            pltpu.VMEM((packed, groups * HEAD_SIZE), jnp.bfloat16),
            pltpu.VMEM((packed, 2 * groups * HEAD_SIZE), jnp.bfloat16),
            pltpu.VMEM((HEAD_SIZE + FLAG_COLUMNS, group_length * queries), jnp.float32),
            pltpu.VMEM((8, group_length * queries), jnp.float32),
        ],
        compiler_params=pltpu.CompilerParams(vmem_limit_bytes=40 * 1024 * 1024),
        cost_estimate=pl.CostEstimate(
            flops=8 * HEAD_SIZE * pairs, bytes_accessed=8 * 1024 * 1024, transcendentals=pairs
        ),
        name="window_attention",
    )(counts_here, queries_t, *blocks)


def per_device(tokens, norm_gain, w_query, key_weight, value_weight, w_out, counts):
    rows, half_width = tokens.shape
    layer_total = norm_gain.shape[0]
    model_width = norm_gain.shape[1]
    span = WINDOW // rows
    groups = key_weight.shape[2] // HEAD_SIZE
    heads = w_query.shape[2] // HEAD_SIZE
    block_index = lax.axis_index("seq")
    head_index = lax.axis_index("head")
    half_dim = HEAD_SIZE // 2
    swap = lambda i: lax.axis_size("head") - 1 - i

    places = block_index * rows + jnp.arange(rows, dtype=jnp.int32)
    inverse = jnp.power(
        jnp.float32(rope_base), -2.0 * jnp.arange(half_dim, dtype=jnp.float32) / HEAD_SIZE
    )
    angles = places.astype(jnp.float32)[:, None] * inverse[None, :]
    cosine, sine = lax.optimization_barrier((jnp.cos(angles), jnp.sin(angles)))

    numbers = block_index - jnp.arange(span + 1, dtype=jnp.int32)
    matches = numbers[:, None] == jnp.arange(counts.shape[0], dtype=jnp.int32)[None, :]
    counts_here = jnp.sum(jnp.where(matches, counts[None, :], 0), axis=1)
    counts_here = jnp.concatenate([counts_here, jnp.zeros((1,), jnp.int32)])
    valid = (jnp.arange(rows, dtype=jnp.int32) < counts_here[0])[:, None]

    other = moved(tokens, "head", swap)
    hidden = jnp.where(
        head_index == 0,
        jnp.concatenate([tokens, other], axis=1),
        jnp.concatenate([other, tokens], axis=1),
    )
    scale = math.log2(math.e) / math.sqrt(HEAD_SIZE)
    for layer in range(layer_total):
        widened = hidden.astype(jnp.float32)
        mean_square = jnp.mean(widened * widened, axis=1, keepdims=True)
        normed = (
            widened * lax.rsqrt(mean_square + norm_epsilon) * norm_gain[layer][None, :]
        ).astype(jnp.bfloat16)
        key_raw = jnp.dot(normed, key_weight[layer], preferred_element_type=jnp.float32)
        value_raw = jnp.dot(normed, value_weight[layer], preferred_element_type=jnp.float32)
        pieces = []
        for g in range(groups):
            a = key_raw[:, g * HEAD_SIZE : g * HEAD_SIZE + half_dim]
            b = key_raw[:, g * HEAD_SIZE + half_dim : (g + 1) * HEAD_SIZE]
            pieces += [a * cosine - b * sine, b * cosine + a * sine]
        keys = jnp.concatenate(pieces, axis=1)
        keys = jnp.where(valid, keys, keys[0:1])
        values = jnp.where(valid, value_raw, 0.0)
        own = jnp.concatenate([keys.astype(jnp.bfloat16), values.astype(jnp.bfloat16)], axis=1)
        blocks = spread_blocks(own, span)

        query_raw = lax.dot_general(
            w_query[layer], normed, (((0,), (1,)), ((), ())), preferred_element_type=jnp.float32
        ).reshape(heads, 2, half_dim, rows)
        a, b = query_raw[:, 0], query_raw[:, 1]
        cosine_t, sine_t = (cosine.T * scale)[None], (sine.T * scale)[None]
        queries_t = (
            jnp.stack([a * cosine_t - b * sine_t, b * cosine_t + a * sine_t], axis=1)
            .astype(jnp.bfloat16)
            .reshape(heads * HEAD_SIZE, rows)
        )
        attended_t = attend(queries_t, blocks, counts_here, groups)
        partial = lax.dot_general(
            attended_t, w_out[layer], (((0,), (0,)), ((), ())), preferred_element_type=jnp.float32
        ).astype(jnp.bfloat16)
        if layer < layer_total - 1:
            theirs = moved(partial, "head", swap)
            branch = partial.astype(jnp.float32) + theirs.astype(jnp.float32)
            hidden = (widened + branch).astype(jnp.bfloat16)
        else:
            mine = lax.dynamic_slice_in_dim(partial, head_index * half_width, half_width, 1)
            sent = lax.dynamic_slice_in_dim(partial, (1 - head_index) * half_width, half_width, 1)
            theirs = moved(sent, "head", swap)
            kept = lax.dynamic_slice_in_dim(hidden, head_index * half_width, half_width, 1)
            branch = mine.astype(jnp.float32) + theirs.astype(jnp.float32)
            hidden = (kept.astype(jnp.float32) + branch).astype(jnp.bfloat16)
    return hidden


def solution(mesh):
    return jax.shard_map(
        per_device,
        mesh=mesh,
        in_specs=(
            P("seq", "head"),
            P(),
            P(None, None, "head"),
            P(None, None, "head"),
            P(None, None, "head"),
            P(None, "head", None),
            P(),
        ),
        out_specs=P("seq", "head"),
        check_vma=False,
    )
```

```python
import functools
import math

import jax
import jax.numpy as jnp
from jax import lax
from jax.experimental import pallas as pl
from jax.experimental.pallas import tpu as pltpu
from jax.sharding import PartitionSpec as P

HEAD_SIZE = 128
WINDOW = 4096
CHUNKS = 2
KEY_TILE = 512
FLAG_COLUMNS = 16

norm_epsilon = 1e-05
rope_base = 10000.0


def moved(value, axis, target_of):
    count = lax.axis_size(axis)
    pairs = [(source, target_of(source)) for source in range(count)]
    return lax.ppermute(value, axis, [(a, b) for a, b in pairs if 0 <= b < count])


def spread_blocks(own, span):
    if span != 8 or lax.axis_size("seq") % 4:
        blocks = [own]
        for _ in range(span):
            blocks.append(moved(blocks[-1], "seq", lambda i: i + 1))
        return blocks
    index = lax.axis_index("seq")
    low_chip = index % 4 < 2
    first_core = index % 2 == 0
    pick_chip = lambda a, b: jnp.where(low_chip, a, b)
    pick_core = lambda a, b: jnp.where(first_core, a, b)
    across = lambda i: i + 2 if i % 4 < 2 else i - 2
    beside = lambda i: i + 1 if i % 2 == 0 else i - 1
    four = moved(own, "seq", lambda i: i + 4)
    eight = moved(own, "seq", lambda i: i + 8)
    two = moved(pick_chip(own, four), "seq", across)
    six = moved(pick_chip(four, eight), "seq", across)
    one = moved(pick_core(own, two), "seq", beside)
    three = moved(pick_core(two, four), "seq", beside)
    five = moved(pick_core(four, six), "seq", beside)
    seven = moved(pick_core(six, eight), "seq", beside)
    return [own, one, two, three, four, five, six, seven, eight]


def attention_kernel(span, chunks, groups, group_length, part, *refs):
    counts_ref, q_ref = refs[:2]
    total_blocks = (1 + span) * chunks
    blocks = refs[2 : 2 + total_blocks]
    o_ref, kp, vp, acc, top = refs[2 + total_blocks :]
    rows, queries = blocks[0].shape[0], q_ref.shape[1]
    width = groups * HEAD_SIZE
    offset = jnp.int32(0)

    def flags(count, columns):
        places = lax.broadcasted_iota(jnp.int32, (rows, columns), 0)
        return (places < count).astype(jnp.float32).astype(jnp.bfloat16)

    def store(at, size, keys, values, flag):
        where = pl.ds(pl.multiple_of(at, 16), size)
        kp[where, :] = keys
        for g in range(groups):
            vp[where, 2 * g * HEAD_SIZE : (2 * g + 1) * HEAD_SIZE] = values(g)
            vp[where, (2 * g + 1) * HEAD_SIZE : (2 * g + 2) * HEAD_SIZE] = flag

    for b in range(chunks, span * chunks):
        count = counts_ref[b]
        store(
            offset,
            rows,
            blocks[b][:, :width],
            lambda g: blocks[b][:, width + g * HEAD_SIZE : width + (g + 1) * HEAD_SIZE],
            flags(count, HEAD_SIZE),
        )
        offset = offset + ((count + 15) // 16) * 16
    blank = jnp.zeros((KEY_TILE, HEAD_SIZE), jnp.bfloat16)
    store(
        offset,
        KEY_TILE,
        jnp.broadcast_to(blocks[0][0:1, :width], (KEY_TILE, width)),
        lambda g: blank,
        blank,
    )
    tiles = (offset + KEY_TILE - 1) // KEY_TILE
    key_place = lax.broadcasted_iota(jnp.int32, (rows, queries), 0)
    query_place = lax.broadcasted_iota(jnp.int32, (rows, queries), 1)

    @pl.loop(0, groups)
    def _(g):
        lanes = pl.ds(pl.multiple_of(g * HEAD_SIZE, HEAD_SIZE), HEAD_SIZE)
        value_lanes = pl.ds(pl.multiple_of(width + g * HEAD_SIZE, HEAD_SIZE), HEAD_SIZE)
        flagged_lanes = pl.ds(
            pl.multiple_of(2 * g * HEAD_SIZE, HEAD_SIZE), HEAD_SIZE + FLAG_COLUMNS
        )

        def head_rows(head):
            first = (g * group_length + head) * HEAD_SIZE
            return pl.ds(pl.multiple_of(first, HEAD_SIZE), HEAD_SIZE)

        def step(keys, values, mask):
            for head in range(group_length):
                spot = slice(head * queries, (head + 1) * queries)
                scores = jnp.dot(keys, q_ref[head_rows(head), :], preferred_element_type=jnp.float32)
                if mask is not None:
                    scores = jnp.where(mask, scores, -jnp.inf)
                before = top[0:1, spot]
                after = jnp.maximum(before, jnp.max(scores, axis=0, keepdims=True))
                weights = jnp.exp2(scores - after).astype(jnp.bfloat16)
                fade = jnp.exp2(before - after)
                added = lax.dot_general(
                    values, weights, (((0,), (0,)), ((), ())), preferred_element_type=jnp.float32
                )
                acc[:, spot] = acc[:, spot] * fade + added
                top[0:1, spot] = after

        def edge(b, mask):
            values = jnp.concatenate(
                [blocks[b][:, value_lanes], flags(counts_ref[b], FLAG_COLUMNS)], axis=1
            )
            step(blocks[b][:, lanes], values, mask)

        acc[...] = jnp.zeros_like(acc)
        top[...] = jnp.full_like(top, -jnp.inf)
        for b in range(part):

            @pl.when(counts_ref[b] > 0)
            def _():
                edge(b, None)

        inside = key_place < counts_ref[part]
        edge(part, inside & (key_place <= query_place))

        @pl.loop(0, tiles)
        def _(i):
            where = pl.ds(pl.multiple_of(i * KEY_TILE, KEY_TILE), KEY_TILE)
            step(kp[where, lanes], vp[where, flagged_lanes], None)

        for b in range(part, chunks):
            last = span * chunks + b

            @pl.when(counts_ref[last] > 0)
            def _():
                valid = key_place < counts_ref[last]
                edge(last, (valid & (key_place > query_place)) if b == part else valid)

        for head in range(group_length):
            spot = slice(head * queries, (head + 1) * queries)
            total = acc[HEAD_SIZE : HEAD_SIZE + 1, spot]
            o_ref[head_rows(head), :] = (acc[:HEAD_SIZE, spot] / total).astype(jnp.bfloat16)


def attend(queries_t, blocks, counts_here, groups, chunks, part):
    span = len(blocks) // chunks - 1
    rows = blocks[0].shape[0]
    queries = queries_t.shape[1]
    group_length = queries_t.shape[0] // HEAD_SIZE // groups
    packed = (span - 1) * chunks * rows + KEY_TILE
    vmem = pl.BlockSpec(memory_space=pltpu.VMEM)
    pairs = queries * span * chunks * rows * group_length * groups
    return pl.pallas_call(
        functools.partial(attention_kernel, span, chunks, groups, group_length, part),
        out_shape=jax.ShapeDtypeStruct(queries_t.shape, jnp.bfloat16),
        in_specs=[pl.BlockSpec(memory_space=pltpu.SMEM)] + [vmem] * (1 + len(blocks)),
        out_specs=vmem,
        scratch_shapes=[
            pltpu.VMEM((packed, groups * HEAD_SIZE), jnp.bfloat16),
            pltpu.VMEM((packed, 2 * groups * HEAD_SIZE), jnp.bfloat16),
            pltpu.VMEM((HEAD_SIZE + FLAG_COLUMNS, group_length * queries), jnp.float32),
            pltpu.VMEM((8, group_length * queries), jnp.float32),
        ],
        compiler_params=pltpu.CompilerParams(vmem_limit_bytes=32 * 1024 * 1024),
        cost_estimate=pl.CostEstimate(
            flops=16 * HEAD_SIZE * pairs, bytes_accessed=8 * 1024 * 1024, transcendentals=pairs
        ),
        name="window_attention_" + str(part),
    )(counts_here, queries_t, *blocks)


def per_device(tokens, norm_gain, w_query, key_weight, value_weight, w_out, counts):
    rows, half_width = tokens.shape
    layer_total = norm_gain.shape[0]
    span = WINDOW // rows
    chunks = CHUNKS
    piece = rows // chunks
    groups = key_weight.shape[2] // HEAD_SIZE
    heads = w_query.shape[2] // HEAD_SIZE
    block_index = lax.axis_index("seq")
    head_index = lax.axis_index("head")
    half_dim = HEAD_SIZE // 2
    swap = lambda i: lax.axis_size("head") - 1 - i
    scale = math.log2(math.e) / math.sqrt(HEAD_SIZE)

    places = (block_index * rows + jnp.arange(rows, dtype=jnp.int32)).astype(jnp.float32)
    inverse = jnp.power(
        jnp.float32(rope_base), -2.0 * jnp.arange(half_dim, dtype=jnp.float32) / HEAD_SIZE
    )
    angles = places[:, None] * inverse[None, :]
    angles_t = inverse[:, None] * places[None, :]
    cosine, sine, cosine_t, sine_t = lax.optimization_barrier(
        (jnp.cos(angles), jnp.sin(angles), jnp.cos(angles_t) * scale, jnp.sin(angles_t) * scale)
    )

    numbers = block_index - jnp.arange(span + 1, dtype=jnp.int32)
    matches = numbers[:, None] == jnp.arange(counts.shape[0], dtype=jnp.int32)[None, :]
    counts_here = jnp.sum(jnp.where(matches, counts[None, :], 0), axis=1)
    starts = piece * jnp.arange(chunks, dtype=jnp.int32)
    counts_here = jnp.clip(counts_here[:, None] - starts[None, :], 0, piece).reshape(-1)

    def joined(kept, partial, theirs):
        branch = partial.astype(jnp.float32) + theirs.astype(jnp.float32)
        return (kept.astype(jnp.float32) + branch).astype(jnp.bfloat16)

    hidden = []
    for c in range(chunks):
        own = tokens[c * piece : (c + 1) * piece]
        other = moved(own, "head", swap)
        hidden.append(
            jnp.where(
                head_index == 0,
                jnp.concatenate([own, other], axis=1),
                jnp.concatenate([other, own], axis=1),
            )
        )
    for layer in range(layer_total):
        blocks = [None] * ((span + 1) * chunks)
        queries_t = []
        for c in range(chunks):
            here = slice(c * piece, (c + 1) * piece)
            if layer and c:
                kept, partial, theirs = arrived[c]
                near = min(2, span) * chunks + c - 1
                theirs, blocks[near], queries_t[c - 1] = lax.optimization_barrier(
                    (theirs, blocks[near], queries_t[c - 1])
                )
                hidden[c] = joined(kept, partial, theirs)
            widened = hidden[c].astype(jnp.float32)
            mean_square = jnp.mean(widened * widened, axis=1, keepdims=True)
            normed = (
                widened * lax.rsqrt(mean_square + norm_epsilon) * norm_gain[layer][None, :]
            ).astype(jnp.bfloat16)
            key_raw = jnp.dot(normed, key_weight[layer], preferred_element_type=jnp.float32)
            value_raw = jnp.dot(normed, value_weight[layer], preferred_element_type=jnp.float32)
            pieces = []
            for g in range(groups):
                a = key_raw[:, g * HEAD_SIZE : g * HEAD_SIZE + half_dim]
                b = key_raw[:, g * HEAD_SIZE + half_dim : (g + 1) * HEAD_SIZE]
                pieces += [
                    a * cosine[here] - b * sine[here],
                    b * cosine[here] + a * sine[here],
                ]
            valid = (jnp.arange(piece, dtype=jnp.int32) < counts_here[c])[:, None]
            keys = jnp.concatenate(pieces, axis=1)
            keys = jnp.where(valid, keys, keys[0:1])
            values = jnp.where(valid, value_raw, 0.0)
            own = jnp.concatenate([keys.astype(jnp.bfloat16), values.astype(jnp.bfloat16)], axis=1)
            blocks[c::chunks] = spread_blocks(own, span)
            query_raw = lax.dot_general(
                w_query[layer], normed, (((0,), (1,)), ((), ())), preferred_element_type=jnp.float32
            ).reshape(heads, 2, half_dim, piece)
            a, b = query_raw[:, 0], query_raw[:, 1]
            cosine_here, sine_here = cosine_t[None, :, here], sine_t[None, :, here]
            queries_t.append(
                jnp.stack(
                    [a * cosine_here - b * sine_here, b * cosine_here + a * sine_here], axis=1
                )
                .astype(jnp.bfloat16)
                .reshape(heads * HEAD_SIZE, piece)
            )
        following, arrived = [], [None] * chunks
        for c in range(chunks):
            query_now = queries_t[c]
            if c:
                query_now, partial = lax.optimization_barrier((query_now, partial))
                following[-1] = partial
            attended_t = attend(query_now, blocks, counts_here, groups, chunks, c)
            partial = lax.dot_general(
                attended_t, w_out[layer], (((0,), (0,)), ((), ())), preferred_element_type=jnp.float32
            ).astype(jnp.bfloat16)
            following.append(partial)
        for c in range(chunks):
            partial = following[c]
            if layer < layer_total - 1:
                theirs = moved(partial, "head", swap)
                kept = hidden[c]
            else:
                take = lambda x, i: lax.dynamic_slice_in_dim(x, i * half_width, half_width, 1)
                theirs = moved(take(partial, 1 - head_index), "head", swap)
                kept = take(hidden[c], head_index)
                partial = take(partial, head_index)
            arrived[c] = (kept, partial, theirs)
        hidden = [joined(*entry) for entry in arrived]
    return jnp.concatenate(hidden, axis=0)


def solution(mesh):
    return jax.shard_map(
        per_device,
        mesh=mesh,
        in_specs=(
            P("seq", "head"),
            P(),
            P(None, None, "head"),
            P(None, None, "head"),
            P(None, None, "head"),
            P(None, "head", None),
            P(),
        ),
        out_specs=P("seq", "head"),
        check_vma=False,
    )
```
